32 devices in a mesh: row: 8 (over z, core), col: 4 (over y, x).
Axes of the slice: x: 2, y: 2, z: 4, core: 2. Of those that a mesh axis runs over, the one named last changes fastest.
Arguments:
- covariance: float32 [8192, 8192], P('row', 'col'), as said below
- state_mean: float32 [8192], P('row'), may hold values from -6 to 6
- obs_values: float32 [2, 256], replicated, may hold values from -8 to 8
- obs_cells: int32 [2, 4, 256], replicated, may hold values from 0 to 8191
- obs_weights: float32 [2, 4, 256], replicated, may hold values from 0.2 to 1
- obs_variance: float32 [2, 256], replicated, may hold values from 0.05 to 1
Outputs:
- covariance_after: float32 [8192, 8192], P('row', 'col')
- state_after: float32 [8192], P('row')
The draws below stay inside these ranges and needn't reach their ends.
Inputs may be any that keep to these rules, and one draw needn't show every extreme that they name: `covariance`: symmetric and positive definite.
All inputs are finite; a program needn't handle non-finite values.
Results may differ from the reference program's by a relative error of at most 0.0001.
Values sent between devices are 32-bit elements; how exact they have to be, the bound alone decides.
A program may use at most 64 MiB of HBM per device.

```python
import math
import jax
import jax.numpy as jnp
from jax import lax

STATE = 8192
OBS = 256
FOOT = 4
BATCHES = 2


def draw_covariance(key, part):
    noise = jax.random.normal(jax.random.fold_in(key, 11), (STATE, STATE), jnp.float32)
    sym = (noise + noise.T) * (0.35 / math.sqrt(STATE))
    diag = jax.random.uniform(jax.random.fold_in(key, 12), (STATE,), jnp.float32, 1.5, 2.5)
    matrix = sym + jnp.diag(diag)
    return matrix


def place_ends(drawn, own_key, least, high):
    shape = drawn.shape
    spot = [jax.random.randint(jax.random.fold_in(own_key, axis), (), 0, shape[axis]) for axis in range(len(shape))]
    drawn = drawn.at[tuple(spot)].set(least)
    longest = shape.index(max(shape))
    spot[longest] = (spot[longest] + 1) % shape[longest]
    return drawn.at[tuple(spot)].set(high)


def block_levels(key, shape, split, smallest, top_value):
    level, own = 1.0, jax.random.fold_in(key, 6)
    for position, blocks in split:
        steps = jnp.exp(jax.random.uniform(jax.random.fold_in(own, position), (blocks,), jnp.float32, smallest / len(split), top_value / len(split)))
        level = level * jnp.repeat(steps, shape[position] // blocks).reshape([-1 if axis == position else 1 for axis in range(len(shape))])
    return level


def bell_draw(rng, shape, scale, limit, shards=(), kind=jnp.bfloat16):
    array = jax.random.normal(rng, shape, jnp.float32) * scale
    if len(shards) > 0:
        array = block_levels(rng, shape, shards, -0.22, 0.18) * array
    return jnp.clip(array, min=-limit, max=limit).astype(kind)


def setup_inputs(seed: int = 0) -> dict:
    seeds = jax.random.split(jax.random.key(seed), 7)
    covariance = draw_covariance(jax.random.fold_in(seeds[6], 71), 0)
    state_mean = bell_draw(seeds[1], (STATE,), 1.0, 6.0, ((0, 8),), jnp.float32)
    obs_values = bell_draw(seeds[2], (BATCHES, OBS), 2.0, 8.0, (), jnp.float32)
    obs_cells = place_ends(jax.random.randint(seeds[3], (BATCHES, FOOT, OBS), 0, STATE), jax.random.fold_in(seeds[3], 1), 0, STATE - 1).astype(jnp.int32)
    obs_weights = jnp.clip(jax.random.uniform(seeds[4], (BATCHES, FOOT, OBS), jnp.float32, 0.2, 1.0), 0.2, 1.0)
    obs_variance = jnp.clip(jnp.exp(jax.random.uniform(seeds[5], (BATCHES, OBS), jnp.float32, math.log(0.05), math.log(1.0))), 0.05, 1.0)
    return {"covariance": covariance, "state_mean": state_mean, "obs_values": obs_values, "obs_cells": obs_cells, "obs_weights": obs_weights, "obs_variance": obs_variance}


def reference(covariance, state_mean, obs_values, obs_cells, obs_weights, obs_variance):
    hi = lax.Precision.HIGHEST
    matrix = covariance
    mean = state_mean
    for batch in range(BATCHES):
        cells = obs_cells[batch]
        weights = obs_weights[batch]
        cross = jnp.zeros((STATE, OBS), jnp.float32)
        for foot in range(FOOT):
            cross = cross + matrix[:, cells[foot]] * weights[foot][None, :]
        inner = jnp.zeros((OBS, OBS), jnp.float32)
        predicted = jnp.zeros((OBS,), jnp.float32)
        for foot in range(FOOT):
            inner = inner + weights[foot][:, None] * cross[cells[foot], :]
            predicted = predicted + weights[foot] * mean[cells[foot]]
        inner = 0.5 * (inner + inner.T) + jnp.diag(obs_variance[batch])
        factor = jnp.linalg.cholesky(inner)
        gain = lax.linalg.triangular_solve(factor, cross.T, left_side=True, lower=True).T
        innov = (obs_values[batch] - predicted)[:, None]
        white = lax.linalg.triangular_solve(factor, innov, left_side=True, lower=True)[:, 0]
        mean = mean + jnp.dot(gain.astype(jnp.float32), white.astype(jnp.float32), precision=hi, preferred_element_type=jnp.float32)
        matrix = matrix - jnp.dot(gain.astype(jnp.float32), gain.T.astype(jnp.float32), precision=hi, preferred_element_type=jnp.float32)
    return (matrix, mean)
```

```python
import jax
import jax.numpy as jnp
from jax import lax
from jax.sharding import PartitionSpec as P

HI = lax.Precision.HIGHEST
MID = lax.Precision.HIGH


def dot(a, b, precision):
    return jnp.dot(a, b, precision=precision, preferred_element_type=jnp.float32)


def local_operator(cells, weights, start, count):
    positions = start + lax.iota(jnp.int32, count)[:, None]
    total = jnp.zeros((count, cells.shape[1]), jnp.float32)
    for foot in range(cells.shape[0]):
        total = total + jnp.where(cells[foot][None, :] == positions, weights[foot][None, :], 0.0)
    return total


def on_device(covariance, state_mean, obs_values, obs_cells, obs_weights, obs_variance):
    rows_dev, cols_dev = covariance.shape
    row_index = lax.axis_index("row")
    col_index = lax.axis_index("col")
    ratio = lax.axis_size("row") // lax.axis_size("col")
    batches, foot, width = obs_cells.shape
    total = batches * width
    cells = obs_cells.transpose(1, 0, 2).reshape(foot, total)
    weights = obs_weights.transpose(1, 0, 2).reshape(foot, total)
    values = obs_values.reshape(total)
    variance = obs_variance.reshape(total)
    col_op = local_operator(cells, weights, col_index * cols_dev, cols_dev)
    row_op = local_operator(cells, weights, row_index * rows_dev, rows_dev)
    part = dot(covariance, col_op, MID)
    part_inner = dot(row_op.T, part, MID)
    part_pred = dot(row_op.T, state_mean[:, None], HI)
    part_pred = jnp.where(col_index == 0, part_pred, 0.0)
    stacked = jnp.concatenate([part_inner, jnp.broadcast_to(part_pred, (total, 128))], axis=1)
    stacked = lax.psum(stacked, ("row", "col"))
    part, stacked = lax.optimization_barrier((part, stacked))
    cross = lax.psum(part, "col")
    pieces = []
    for step in range(ratio):
        mine = row_index == col_index * ratio + step
        pieces.append(jnp.where(mine, cross, 0.0))
    cross_cols = jnp.concatenate(lax.psum(pieces, "row"), axis=0)
    inner = stacked[:, :total]
    inner = 0.5 * (inner + inner.T) + jnp.diag(variance)
    innov = values - stacked[:, total]
    factor = jnp.linalg.cholesky(inner)
    eye = jnp.eye(total, dtype=jnp.float32)
    inverse = lax.linalg.triangular_solve(factor, eye, left_side=True, lower=True)
    white = dot(inverse, innov[:, None], HI)
    gain = dot(cross, inverse.T, MID)
    gain_cols = dot(cross_cols, inverse.T, MID)
    mean = state_mean + dot(gain, white, HI)[:, 0]
    matrix = covariance - dot(gain, gain_cols.T, MID)
    return (matrix, mean)


def solution(mesh):
    return jax.shard_map(
        on_device,
        mesh=mesh,
        in_specs=(P("row", "col"), P("row"), P(), P(), P(), P()),
        out_specs=(P("row", "col"), P("row")),
        check_vma=False,
    )
```

```python
import functools

import jax
import jax.numpy as jnp
from jax import lax
from jax.experimental import pallas as pl
from jax.experimental.pallas import tpu as pltpu
from jax.sharding import PartitionSpec as P

HI = lax.Precision.HIGHEST
MID = lax.Precision.HIGH
MESH = pl.DeviceIdType.MESH
BLK = 128
SUB = 8

def base_inverse(work, cols):
    def panel_step(g, carry):
        start = pl.multiple_of(g * SUB, SUB)
        panel = work[pl.ds(start, SUB), :]
        cols[:, :SUB] = panel[:, :BLK].T
        square = cols[pl.ds(start, SUB), :SUB]
        wide = [jnp.broadcast_to(square[:, j : j + 1], (SUB, BLK)) for j in range(SUB)]
        left, right = panel[:, :BLK], panel[:, BLK:]
        below = lax.broadcasted_iota(jnp.int32, (SUB, BLK), 0)
        scale = jnp.zeros((SUB, BLK), jnp.float32)
        for j in range(SUB):
            pivot = jnp.broadcast_to(wide[j][j : j + 1, :], (SUB, BLK))
            inv = 1.0 / pivot
            scale = jnp.where(below == j, lax.rsqrt(pivot), scale)
            ratio = jnp.where(below > j, wide[j] * inv, 0.0)
            left = left - ratio * left[j : j + 1, :]
            right = right - ratio * right[j : j + 1, :]
            for k in range(j + 1, SUB):
                wide[k] = wide[k] - ratio * wide[k][j : j + 1, :]
        left = left * scale
        right = right * scale
        both = jnp.concatenate([left, right], axis=1)
        lane = lax.broadcasted_iota(jnp.int32, (SUB, BLK), 1)
        lhs = jnp.where(lane >= start + SUB, left, 0.0)
        work[pl.ds(start, SUB), :] = both
        work[...] = work[...] - lax.dot_general(lhs, both, (((0,), (0,)), ((), ())), precision=HI, preferred_element_type=jnp.float32)
        return carry
    lax.fori_loop(0, BLK // SUB, panel_step, 0)

def factor_inverse(mat, work, cols, between):
    size = mat.shape[0]
    eye = (lax.broadcasted_iota(jnp.int32, (BLK, BLK), 0) == lax.broadcasted_iota(jnp.int32, (BLK, BLK), 1)).astype(jnp.float32)
    for b in range(size // BLK):
        lo, hi = b * BLK, (b + 1) * BLK
        work[:, :BLK] = mat[lo:hi, lo:hi]
        work[:, BLK:] = eye
        base_inverse(work, cols)
        winv = work[:, BLK:]
        if hi < size:
            panel = jnp.dot(winv, mat[lo:hi, hi:size], precision=HI, preferred_element_type=jnp.float32)
        if lo > 0:
            left = jnp.dot(winv, mat[lo:hi, size : size + lo], precision=HI, preferred_element_type=jnp.float32)
            mat[lo:hi, size : size + lo] = left
        mat[lo:hi, size + lo : size + hi] = winv
        if hi < size:
            right = mat[lo:hi, size : size + hi]
            dims = (((0,), (0,)), ((), ()))
            mat[hi:size, hi:size] = mat[hi:size, hi:size] - lax.dot_general(panel, panel, dims, precision=HI, preferred_element_type=jnp.float32)
            mat[hi:size, size : size + hi] = mat[hi:size, size : size + hi] - lax.dot_general(panel, right, dims, precision=HI, preferred_element_type=jnp.float32)
        between(b)


def pair_blocks(size):
    count = size // BLK
    return [(i, j) for i in range(count) for j in range(i + 1)]


def kernel(
    nr, nc, s_ref, t_ref, var_ref, inv_ref, xr_ref, xc_ref, pred_ref,
    acc, full, land, tland, mat, work, cols, send_sem, recv_sem,
):
    ratio = nr // nc
    row, col = lax.axis_index("row"), lax.axis_index("col")
    high, low = row // ratio, row % ratio
    packed = s_ref.shape[0]
    rows, size = t_ref.shape
    chunk = rows // nc
    used = [0]

    def take(count):
        used[0] += count
        return used[0] - count

    levels = [
        (ratio, low, lambda d: (high * ratio + lax.rem(low + d, ratio), col)),
        (nc, col, lambda d: (row, lax.rem(col + d, nc))),
        (nc, high, lambda d: (lax.rem(high + d, nc) * ratio + low, col)),
    ]
    barrier = pltpu.get_barrier_semaphore()
    for n, me, peer in levels:
        for d in range(1, n):
            pl.semaphore_signal(barrier, inc=1, device_id=peer(d), device_id_type=MESH)
    pl.semaphore_wait(barrier, ratio - 1 + 2 * (nc - 1))

    def remote(src, dst, sem, device):
        return pltpu.make_async_remote_copy(
            src_ref=src, dst_ref=dst, send_sem=send_sem.at[sem], recv_sem=recv_sem.at[sem],
            device_id=device, device_id_type=MESH,
        )

    acc[...] = s_ref[...]
    start, length, slot = 0, packed, 0
    spots = []
    for level, (n, me, peer) in enumerate(levels):
        part = length // n
        base = take(n - 1)
        copies = []
        for d in range(1, n):
            other = lax.rem(me + d, n)
            src = (s_ref if level == 0 else acc).at[pl.ds(pl.multiple_of(start + other * part, 8), part)]
            dst = land.at[pl.ds(slot + (d - 1) * part, part)]
            copies.append(remote(src, dst, base + d - 1, peer(d)))
            copies[-1].start()
        start = pl.multiple_of(start + me * part, 8)
        length = part
        spots.append((start, part))
        for copy in copies:
            copy.wait()
        mine = acc[pl.ds(start, part), :]
        for d in range(1, n):
            mine = mine + land[pl.ds(slot + (d - 1) * part, part), :]
        acc[pl.ds(start, part), :] = mine
        slot += (n - 1) * part
    full[pl.ds(start, length), :] = acc[pl.ds(start, length), :]

    t_base = take(nc - 1)
    _, _, col_peer = levels[1]
    t_copies = []
    for d in range(1, nc):
        other = lax.rem(col + d, nc)
        src = t_ref.at[pl.ds(pl.multiple_of(other * chunk, 8), chunk)]
        t_copies.append(remote(src, tland.at[d - 1], t_base + d - 1, col_peer(d)))

    for level in (2, 1, 0):
        n, me, peer = levels[level]
        begin, part = spots[level]
        base = take(n - 1)
        copies = []
        for d in range(1, n):
            where = full.at[pl.ds(begin, part)]
            copies.append(remote(where, where, base + d - 1, peer(d)))
            copies[-1].start()
        if level == 1:
            for copy in t_copies:
                copy.start()
        for copy in copies:
            copy.wait()

    same = lax.broadcasted_iota(jnp.int32, (BLK, BLK), 0) == lax.broadcasted_iota(jnp.int32, (BLK, BLK), 1)
    for index, (i, j) in enumerate(pair_blocks(size)):
        block = full[index * BLK : (index + 1) * BLK, :]
        if i == j:
            block = block + jnp.where(same, var_ref[:, i * BLK : (i + 1) * BLK], 0.0)
        mat[i * BLK : (i + 1) * BLK, j * BLK : (j + 1) * BLK] = block
        if i != j:
            mat[j * BLK : (j + 1) * BLK, i * BLK : (i + 1) * BLK] = block.T
    mat[:, size:] = jnp.zeros((size, size), jnp.float32)
    tail = len(pair_blocks(size)) * BLK
    pred_ref[...] = full[tail : tail + 8, :]

    gather_base = take(nc - 1)
    chain_base = take(nc)
    down_base = take(nc)
    sib_base = take(nc * (ratio - 1))
    own = xr_ref.at[pl.ds(pl.multiple_of(col * chunk, 8), chunk)]
    gathers = [remote(own, own, gather_base + d - 1, col_peer(d)) for d in range(1, nc)]
    _, _, low_peer = levels[0]
    source = high == col
    top = nc - 1
    above = (jnp.minimum(high + 1, top) * ratio + low, col)
    below = (jnp.maximum(high - 1, 0) * ratio + low, col)
    goes_up = jnp.logical_and(high >= col, high < top)
    goes_down = jnp.logical_and(high <= col, high > 0)

    def gathered():
        for copy in t_copies:
            copy.wait()
        total = t_ref[pl.ds(pl.multiple_of(col * chunk, 8), chunk), :]
        for d in range(1, nc):
            total = total + tland[d - 1]
        xr_ref[pl.ds(pl.multiple_of(col * chunk, 8), chunk), :] = total
        for copy in gathers:
            copy.start()

    def links(d, src_is_own):
        begin = pl.multiple_of(lax.rem(col - d + nc, nc) * chunk, 8)
        dst = xc_ref.at[low, pl.ds(begin, chunk)]
        src = xr_ref.at[pl.ds(begin, chunk)] if src_is_own else dst
        up = remote(src, dst, chain_base + d, above)
        down = pltpu.make_async_remote_copy(
            src_ref=src, dst_ref=dst, send_sem=send_sem.at[down_base + d],
            recv_sem=recv_sem.at[chain_base + d], device_id=below, device_id_type=MESH,
        )
        sibs = [remote(src, dst, sib_base + d * (ratio - 1) + q - 1, low_peer(q)) for q in range(1, ratio)]
        return begin, up, down, sibs

    def relay(d):
        @pl.when(source)
        def _():
            if d > 0:
                gathers[d - 1].wait_recv()
            begin, up, down, sibs = links(d, True)

            @pl.when(goes_up)
            def _():
                up.start()

            @pl.when(goes_down)
            def _():
                down.start()

            for sib in sibs:
                sib.start()
            xc_ref[low, pl.ds(begin, chunk), :] = xr_ref[pl.ds(begin, chunk), :]

        @pl.when(jnp.logical_not(source))
        def _():
            if d > 0:
                gathers[d - 1].wait_recv()
            begin, up, down, sibs = links(d, False)
            up.wait_recv()

            @pl.when(goes_up)
            def _():
                up.start()

            @pl.when(goes_down)
            def _():
                down.start()

            for sib in sibs:
                sib.start()

    def finish():
        for copy in gathers:
            copy.wait_send()
        for d in range(nc):
            _, up, down, sibs = links(d, False)

            @pl.when(goes_up)
            def _():
                up.wait_send()

            @pl.when(goes_down)
            def _():
                down.wait_send()

            for sib in sibs:
                sib.wait()

    def between(b):
        if b == 0:
            gathered()
        elif b < size // BLK - 1:
            relay(b - 1)

    factor_inverse(mat, work, cols, between)
    inv_ref[...] = mat[:, size:]
    for d in range(max(size // BLK - 2, 0), nc):
        relay(d)
    finish()


def exchange(mesh, packed, part, variance):
    nr, nc = mesh.shape["row"], mesh.shape["col"]
    ratio = nr // nc
    rows, size = part.shape
    total = packed.shape[0]
    landing, length = 0, total
    for n in (ratio, nc, nc):
        landing += (n - 1) * (length // n)
        length //= n
    sems = 2 * (ratio - 1 + 2 * (nc - 1)) + 2 * (nc - 1) + 2 * nc + nc * (ratio - 1)
    f32 = jnp.float32
    vmem = pl.BlockSpec(memory_space=pltpu.VMEM)
    return pl.pallas_call(
        functools.partial(kernel, nr, nc),
        out_shape=(
            jax.ShapeDtypeStruct((size, size), f32),
            jax.ShapeDtypeStruct((rows, size), f32),
            jax.ShapeDtypeStruct((ratio, rows, size), f32),
            jax.ShapeDtypeStruct((8, BLK), f32),
        ),
        in_specs=[vmem] * 3,
        out_specs=(vmem,) * 4,
        scratch_shapes=[
            pltpu.VMEM((total, BLK), f32),
            pltpu.VMEM((total, BLK), f32),
            pltpu.VMEM((landing, BLK), f32),
            pltpu.VMEM((nc - 1, rows // nc, size), f32),
            pltpu.VMEM((size, 2 * size), f32),
            pltpu.VMEM((BLK, 2 * BLK), f32),
            pltpu.VMEM((BLK, BLK), f32),
            pltpu.SemaphoreType.DMA((sems,)),
            pltpu.SemaphoreType.DMA((sems,)),
        ],
        compiler_params=pltpu.CompilerParams(collective_id=0, has_side_effects=True, vmem_limit_bytes=40 * 1024 * 1024),
    )(packed, part, variance)


def dot(a, b, precision):
    return jnp.dot(a, b, precision=precision, preferred_element_type=jnp.float32)


def local_operator(cells, weights, start, count):
    positions = start + lax.iota(jnp.int32, count)[:, None]
    total = jnp.zeros((count, cells.shape[1]), jnp.float32)
    for foot in range(cells.shape[0]):
        total = total + jnp.where(cells[foot][None, :] == positions, weights[foot][None, :], 0.0)
    return total


def on_device(mesh, covariance, state_mean, obs_values, obs_cells, obs_weights, obs_variance):
    rows_dev, cols_dev = covariance.shape
    row_index = lax.axis_index("row")
    col_index = lax.axis_index("col")
    devices = mesh.shape["row"] * mesh.shape["col"]
    batches, foot, width = obs_cells.shape
    total = batches * width
    cells = obs_cells.transpose(1, 0, 2).reshape(foot, total)
    weights = obs_weights.transpose(1, 0, 2).reshape(foot, total)
    values = obs_values.reshape(total)
    variance = obs_variance.reshape(1, total)
    col_op = local_operator(cells, weights, col_index * cols_dev, cols_dev)
    row_op = local_operator(cells, weights, row_index * rows_dev, rows_dev)
    part = dot(covariance, col_op, MID)
    part_inner = dot(row_op.T, part, MID)
    part_inner = 0.5 * (part_inner + part_inner.T)
    part_pred = dot(row_op.T, state_mean[:, None], HI)
    part_pred = jnp.where(col_index == 0, part_pred, 0.0)
    pieces = [part_inner[i * BLK : (i + 1) * BLK, j * BLK : (j + 1) * BLK] for i, j in pair_blocks(total)]
    pieces.append(part_pred.reshape(total // BLK, BLK))
    filled = sum(piece.shape[0] for piece in pieces)
    unit = 8 * devices
    pieces.append(jnp.zeros((-(-(filled + 8) // unit) * unit - filled, BLK), jnp.float32))
    packed = jnp.concatenate(pieces, axis=0)
    inverse, cross, cross_cols, pred = exchange(mesh, packed, part, variance)
    predicted = pred[: total // BLK].reshape(total)
    innov = values - predicted
    white = dot(inverse, innov[:, None], HI)
    gain = dot(cross, inverse.T, MID)
    gain_cols = dot(cross_cols.reshape(cols_dev, total), inverse.T, MID)
    mean = state_mean + dot(gain, white, HI)[:, 0]
    matrix = covariance - dot(gain, gain_cols.T, MID)
    return (matrix, mean)


def solution(mesh):
    return jax.shard_map(
        functools.partial(on_device, mesh),
        mesh=mesh,
        in_specs=(P("row", "col"), P("row"), P(), P(), P(), P()),
        out_specs=(P("row", "col"), P("row")),
        check_vma=False,
    )
```

```python
import functools

import jax
import jax.numpy as jnp
from jax import lax
from jax.experimental import pallas as pl
from jax.experimental.pallas import tpu as pltpu
from jax.sharding import PartitionSpec as P

HI = lax.Precision.HIGHEST
MID = lax.Precision.HIGH
MESH = pl.DeviceIdType.MESH
BLK = 128
SUB = 8

def base_inverse(work, cols, midway):
    def panel_step(g, carry):
        start = pl.multiple_of(g * SUB, SUB)
        panel = work[pl.ds(start, SUB), :]
        cols[:, :SUB] = panel[:, :BLK].T
        square = cols[pl.ds(start, SUB), :SUB]
        wide = [jnp.broadcast_to(square[:, j : j + 1], (SUB, BLK)) for j in range(SUB)]
        left, right = panel[:, :BLK], panel[:, BLK:]
        below = lax.broadcasted_iota(jnp.int32, (SUB, BLK), 0)
        scale = jnp.zeros((SUB, BLK), jnp.float32)
        for j in range(SUB):
            pivot = jnp.broadcast_to(wide[j][j : j + 1, :], (SUB, BLK))
            inv = 1.0 / pivot
            scale = jnp.where(below == j, lax.rsqrt(pivot), scale)
            ratio = jnp.where(below > j, wide[j] * inv, 0.0)
            left = left - ratio * left[j : j + 1, :]
            right = right - ratio * right[j : j + 1, :]
            for k in range(j + 1, SUB):
                wide[k] = wide[k] - ratio * wide[k][j : j + 1, :]
        left = left * scale
        right = right * scale
        both = jnp.concatenate([left, right], axis=1)
        lane = lax.broadcasted_iota(jnp.int32, (SUB, BLK), 1)
        lhs = jnp.where(lane >= start + SUB, left, 0.0)
        work[pl.ds(start, SUB), :] = both
        work[...] = work[...] - lax.dot_general(lhs, both, (((0,), (0,)), ((), ())), precision=HI, preferred_element_type=jnp.float32)
        return carry
    half = BLK // SUB // 2
    lax.fori_loop(0, half, panel_step, 0)
    midway()
    lax.fori_loop(half, 2 * half, panel_step, 0)

def factor_inverse(mat, work, cols, between):
    size = mat.shape[0]
    eye = (lax.broadcasted_iota(jnp.int32, (BLK, BLK), 0) == lax.broadcasted_iota(jnp.int32, (BLK, BLK), 1)).astype(jnp.float32)
    for b in range(size // BLK):
        lo, hi = b * BLK, (b + 1) * BLK
        work[:, :BLK] = mat[lo:hi, lo:hi]
        work[:, BLK:] = eye
        base_inverse(work, cols, lambda: between(2 * b))
        winv = work[:, BLK:]
        if hi < size:
            panel = jnp.dot(winv, mat[lo:hi, hi:size], precision=HI, preferred_element_type=jnp.float32)
        if lo > 0:
            left = jnp.dot(winv, mat[lo:hi, size : size + lo], precision=HI, preferred_element_type=jnp.float32)
            mat[lo:hi, size : size + lo] = left
        mat[lo:hi, size + lo : size + hi] = winv
        if hi < size:
            right = mat[lo:hi, size : size + hi]
            dims = (((0,), (0,)), ((), ()))
            mat[hi:size, hi:size] = mat[hi:size, hi:size] - lax.dot_general(panel, panel, dims, precision=HI, preferred_element_type=jnp.float32)
            mat[hi:size, size : size + hi] = mat[hi:size, size : size + hi] - lax.dot_general(panel, right, dims, precision=HI, preferred_element_type=jnp.float32)
        between(2 * b + 1)


def pair_blocks(size):
    count = size // BLK
    return [(i, j) for i in range(count) for j in range(i + 1)]


def kernel(
    nr, nc, t_ref, op_ref, part_ref, var_ref, inv_ref, xr_ref, xc_ref, pred_ref,
    acc, full, land, tland, mat, work, cols, send_sem, recv_sem,
):
    ratio = nr // nc
    row, col = lax.axis_index("row"), lax.axis_index("col")
    high, low = row // ratio, row % ratio
    packed = acc.shape[0]
    rows, size = t_ref.shape
    chunk = rows // nc
    sub = chunk // 2
    pieces = 2 * nc
    used = [0]

    def take(count):
        used[0] += count
        return used[0] - count

    levels = [
        (ratio, low, lambda d: (high * ratio + lax.rem(low + d, ratio), col)),
        (nc, col, lambda d: (row, lax.rem(col + d, nc))),
        (nc, high, lambda d: (lax.rem(high + d, nc) * ratio + low, col)),
    ]
    barrier = pltpu.get_barrier_semaphore()
    for n, me, peer in levels:
        for d in range(1, n):
            pl.semaphore_signal(barrier, inc=1, device_id=peer(d), device_id_type=MESH)
    pl.semaphore_wait(barrier, ratio - 1 + 2 * (nc - 1))

    def remote(src, dst, sem, device):
        return pltpu.make_async_remote_copy(
            src_ref=src, dst_ref=dst, send_sem=send_sem.at[sem], recv_sem=recv_sem.at[sem],
            device_id=device, device_id_type=MESH,
        )

    t_base = take(2 * (nc - 1))
    _, _, col_peer = levels[1]
    t_copies = []
    for h in range(2):
        for d in range(1, nc):
            other = lax.rem(col + d, nc)
            src = t_ref.at[pl.ds(pl.multiple_of(other * chunk + h * sub, 8), sub)]
            dst = tland.at[d - 1, pl.ds(h * sub, sub)]
            t_copies.append(remote(src, dst, t_base + h * (nc - 1) + d - 1, col_peer(d)))
    for copy in t_copies[: nc - 1]:
        copy.start()

    place = 0
    for i in range(size // BLK):
        block = lax.dot_general(
            op_ref[:, i * BLK : (i + 1) * BLK], t_ref[:, : (i + 1) * BLK], (((0,), (0,)), ((), ())),
            precision=MID, preferred_element_type=jnp.float32,
        )
        for j in range(i + 1):
            acc[place : place + BLK, :] = block[:, j * BLK : (j + 1) * BLK]
            place += BLK
    acc[place : place + 8, :] = part_ref[...]
    acc[place + 8 :, :] = jnp.zeros((packed - place - 8, BLK), jnp.float32)
    start, length, slot = 0, packed, 0
    spots = []
    for level, (n, me, peer) in enumerate(levels):
        part = length // n
        base = take(n - 1)
        copies = []
        for d in range(1, n):
            other = lax.rem(me + d, n)
            src = acc.at[pl.ds(pl.multiple_of(start + other * part, 8), part)]
            dst = land.at[pl.ds(slot + (d - 1) * part, part)]
            copies.append(remote(src, dst, base + d - 1, peer(d)))
            copies[-1].start()
        if level == 1:
            for copy in t_copies[nc - 1 :]:
                copy.start()
        start = pl.multiple_of(start + me * part, 8)
        length = part
        spots.append((start, part))
        for copy in copies:
            copy.wait()
        mine = acc[pl.ds(start, part), :]
        for d in range(1, n):
            mine = mine + land[pl.ds(slot + (d - 1) * part, part), :]
        acc[pl.ds(start, part), :] = mine
        slot += (n - 1) * part
    full[pl.ds(start, length), :] = acc[pl.ds(start, length), :]

    for level in (2, 1, 0):
        n, me, peer = levels[level]
        begin, part = spots[level]
        base = take(n - 1)
        copies = []
        for d in range(1, n):
            where = full.at[pl.ds(begin, part)]
            copies.append(remote(where, where, base + d - 1, peer(d)))
            copies[-1].start()
        for copy in copies:
            copy.wait()

    gather_base = take(2 * (nc - 1))
    chain_base = take(pieces)
    down_base = take(pieces)
    sib_base = take(pieces * (ratio - 1))
    gathers = []
    for d in range(1, nc):
        for h in range(2):
            own = xr_ref.at[pl.ds(pl.multiple_of(col * chunk + h * sub, 8), sub)]
            gathers.append(remote(own, own, gather_base + 2 * (d - 1) + h, col_peer(d)))
    _, _, low_peer = levels[0]
    source = high == col
    top = nc - 1
    above = (jnp.minimum(high + 1, top) * ratio + low, col)
    below = (jnp.maximum(high - 1, 0) * ratio + low, col)
    goes_up = jnp.logical_and(high >= col, high < top)
    goes_down = jnp.logical_and(high <= col, high > 0)
    onward = jnp.logical_or(goes_up, goes_down)
    middle = jnp.logical_and(onward, jnp.logical_not(source))
    last = jnp.logical_and(jnp.logical_not(onward), jnp.logical_not(source))

    def links(e, src_is_own):
        begin = pl.multiple_of(lax.rem(col - e // 2 + nc, nc) * chunk + (e % 2) * sub, 8)
        dst = xc_ref.at[low, pl.ds(begin, sub)]
        src = xr_ref.at[pl.ds(begin, sub)] if src_is_own else dst
        up = remote(src, dst, chain_base + e, above)
        down = pltpu.make_async_remote_copy(
            src_ref=src, dst_ref=dst, send_sem=send_sem.at[down_base + e],
            recv_sem=recv_sem.at[chain_base + e], device_id=below, device_id_type=MESH,
        )
        sibs = [remote(src, dst, sib_base + e * (ratio - 1) + q - 1, low_peer(q)) for q in range(1, ratio)]
        return begin, up, down, sibs

    def send_on(up, down, sibs):
        @pl.when(goes_up)
        def _():
            up.start()

        @pl.when(goes_down)
        def _():
            down.start()

        for sib in sibs:
            sib.start()

    def relay_source(e):
        if e >= 2:
            gathers[e - 2].wait_recv()
        begin, up, down, sibs = links(e, True)
        send_on(up, down, sibs)
        xc_ref[low, pl.ds(begin, sub), :] = xr_ref[pl.ds(begin, sub), :]

    def relay_middle(e):
        begin, up, down, sibs = links(e, False)
        up.wait_recv()
        send_on(up, down, sibs)

    def relay_last(e):
        begin, up, down, sibs = links(e, False)
        up.wait_recv()
        for sib in sibs:
            sib.start()

    def between(event):
        @pl.when(source)
        def _():
            if 2 <= event + 1 < pieces:
                relay_source(event + 1)

        @pl.when(middle)
        def _():
            if event < pieces:
                relay_middle(event)

        @pl.when(last)
        def _():
            if 0 <= event - 2 < pieces:
                relay_last(event - 2)

    for copy in t_copies:
        copy.wait()
    where = pl.ds(pl.multiple_of(col * chunk, 8), chunk)
    owned = t_ref[where, :]
    for d in range(1, nc):
        owned = owned + tland[d - 1]
    xr_ref[where, :] = owned

    @pl.when(source)
    def _():
        relay_source(0)
        relay_source(1)

    for copy in gathers:
        copy.start()

    same = lax.broadcasted_iota(jnp.int32, (BLK, BLK), 0) == lax.broadcasted_iota(jnp.int32, (BLK, BLK), 1)
    for index, (i, j) in enumerate(pair_blocks(size)):
        block = full[index * BLK : (index + 1) * BLK, :]
        if i == j:
            block = 0.5 * (block + block.T) + jnp.where(same, var_ref[:, i * BLK : (i + 1) * BLK], 0.0)
        mat[i * BLK : (i + 1) * BLK, j * BLK : (j + 1) * BLK] = block
        if i != j:
            mat[j * BLK : (j + 1) * BLK, i * BLK : (i + 1) * BLK] = block.T
    mat[:, size:] = jnp.zeros((size, size), jnp.float32)
    tail = len(pair_blocks(size)) * BLK
    pred_ref[...] = full[tail : tail + 8, :]

    events = 2 * (size // BLK)
    factor_inverse(mat, work, cols, between)
    inv_ref[...] = mat[:, size:]
    for event in range(events, pieces + 2):
        between(event)
    for copy in gathers:
        copy.wait_send()

    @pl.when(jnp.logical_not(source))
    def _():
        for copy in gathers:
            copy.wait_recv()

    for e in range(pieces):
        _, up, down, sibs = links(e, False)

        @pl.when(goes_up)
        def _():
            up.wait_send()

        @pl.when(goes_down)
        def _():
            down.wait_send()

        for sib in sibs:
            sib.wait()


def exchange(mesh, total, part, row_op, part_pred, variance):
    nr, nc = mesh.shape["row"], mesh.shape["col"]
    ratio = nr // nc
    rows, size = part.shape
    landing, length = 0, total
    for n in (ratio, nc, nc):
        landing += (n - 1) * (length // n)
        length //= n
    sems = 2 * (ratio - 1 + 2 * (nc - 1)) + 4 * (nc - 1) + 4 * nc + 2 * nc * (ratio - 1)
    f32 = jnp.float32
    vmem = pl.BlockSpec(memory_space=pltpu.VMEM)
    return pl.pallas_call(
        functools.partial(kernel, nr, nc),
        out_shape=(
            jax.ShapeDtypeStruct((size, size), f32),
            jax.ShapeDtypeStruct((rows, size), f32),
            jax.ShapeDtypeStruct((ratio, rows, size), f32),
            jax.ShapeDtypeStruct((8, BLK), f32),
        ),
        in_specs=[vmem] * 4,
        out_specs=(vmem,) * 4,
        scratch_shapes=[
            pltpu.VMEM((total, BLK), f32),
            pltpu.VMEM((total, BLK), f32),
            pltpu.VMEM((landing, BLK), f32),
            pltpu.VMEM((nc - 1, rows // nc, size), f32),
            pltpu.VMEM((size, 2 * size), f32),
            pltpu.VMEM((BLK, 2 * BLK), f32),
            pltpu.VMEM((BLK, BLK), f32),
            pltpu.SemaphoreType.DMA((sems,)),
            pltpu.SemaphoreType.DMA((sems,)),
        ],
        compiler_params=pltpu.CompilerParams(collective_id=0, has_side_effects=True, vmem_limit_bytes=40 * 1024 * 1024),
    )(part, row_op, part_pred, variance)


def dot(a, b, precision):
    return jnp.dot(a, b, precision=precision, preferred_element_type=jnp.float32)


def local_operator(cells, weights, start, count):
    positions = start + lax.iota(jnp.int32, count)[:, None]
    total = jnp.zeros((count, cells.shape[1]), jnp.float32)
    for foot in range(cells.shape[0]):
        total = total + jnp.where(cells[foot][None, :] == positions, weights[foot][None, :], 0.0)
    return total


def on_device(mesh, covariance, state_mean, obs_values, obs_cells, obs_weights, obs_variance):
    rows_dev, cols_dev = covariance.shape
    row_index = lax.axis_index("row")
    col_index = lax.axis_index("col")
    devices = mesh.shape["row"] * mesh.shape["col"]
    batches, foot, width = obs_cells.shape
    total = batches * width
    cells = obs_cells.transpose(1, 0, 2).reshape(foot, total)
    weights = obs_weights.transpose(1, 0, 2).reshape(foot, total)
    values = obs_values.reshape(total)
    variance = obs_variance.reshape(1, total)
    col_op = local_operator(cells, weights, col_index * cols_dev, cols_dev)
    row_op = local_operator(cells, weights, row_index * rows_dev, rows_dev)
    part = dot(covariance, col_op, MID)
    part_pred = jnp.sum(row_op * state_mean[:, None], axis=0)
    part_pred = jnp.where(col_index == 0, part_pred, 0.0).reshape(total // BLK, BLK)
    part_pred = jnp.pad(part_pred, ((0, 8 - total // BLK), (0, 0)))
    filled = len(pair_blocks(total)) * BLK + 8
    unit = 8 * devices
    packed = -(-(filled + 8) // unit) * unit
    inverse, cross, cross_cols, pred = exchange(mesh, packed, part, row_op, part_pred, variance)
    predicted = pred[: total // BLK].reshape(total)
    innov = values - predicted
    white = dot(inverse, innov[:, None], HI)
    gain = dot(cross, inverse.T, MID)
    gain_cols = dot(cross_cols.reshape(cols_dev, total), inverse.T, MID)
    mean = state_mean + dot(gain, white, HI)[:, 0]
    matrix = covariance - dot(gain, gain_cols.T, MID)
    return (matrix, mean)


def solution(mesh):
    return jax.shard_map(
        functools.partial(on_device, mesh),
        mesh=mesh,
        in_specs=(P("row", "col"), P("row"), P(), P(), P(), P()),
        out_specs=(P("row", "col"), P("row")),
        check_vma=False,
    )
```

```python
import functools

import jax
import jax.numpy as jnp
from jax import lax
from jax.experimental import pallas as pl
from jax.experimental.pallas import tpu as pltpu
from jax.sharding import PartitionSpec as P

HI = lax.Precision.HIGHEST
MID = lax.Precision.HIGH
MESH = pl.DeviceIdType.MESH
BLK = 128
SUB = 8

def base_inverse(work, cols, midway):
    def panel_step(first, g, carry):
        start = pl.multiple_of(g * SUB, SUB)
        panel = work[pl.ds(start, SUB), :]
        cols[:, :SUB] = panel[:, :BLK].T
        square = cols[pl.ds(start, SUB), :SUB]
        wide = [jnp.broadcast_to(square[:, j : j + 1], (SUB, BLK)) for j in range(SUB)]
        left, right = panel[:, :BLK], panel[:, BLK:]
        below = lax.broadcasted_iota(jnp.int32, (SUB, BLK), 0)
        scale = jnp.zeros((SUB, BLK), jnp.float32)
        for j in range(SUB):
            pivot = jnp.broadcast_to(wide[j][j : j + 1, :], (SUB, BLK))
            inv = 1.0 / pivot
            scale = jnp.where(below == j, lax.rsqrt(pivot), scale)
            ratio = jnp.where(below > j, wide[j] * inv, 0.0)
            left = left - ratio * left[j : j + 1, :]
            right = right - ratio * right[j : j + 1, :]
            for k in range(j + 1, SUB):
                wide[k] = wide[k] - ratio * wide[k][j : j + 1, :]
        left = left * scale
        right = right * scale
        both = jnp.concatenate([left, right], axis=1)
        lane = lax.broadcasted_iota(jnp.int32, (SUB, BLK), 1)
        lhs = jnp.where(lane >= start + SUB, left, 0.0)
        work[pl.ds(start, SUB), :] = both
        work[first:, :] = work[first:, :] - lax.dot_general(lhs[:, first:], both, (((0,), (0,)), ((), ())), precision=HI, preferred_element_type=jnp.float32)
        return carry
    steps = BLK // SUB // 4
    for quarter in range(4):
        if quarter == 2:
            midway()
        first = quarter * steps * SUB
        lax.fori_loop(quarter * steps, (quarter + 1) * steps, functools.partial(panel_step, first), 0)

def factor_inverse(mat, work, cols, between):
    size = mat.shape[0]
    eye = (lax.broadcasted_iota(jnp.int32, (BLK, BLK), 0) == lax.broadcasted_iota(jnp.int32, (BLK, BLK), 1)).astype(jnp.float32)
    for b in range(size // BLK):
        lo, hi = b * BLK, (b + 1) * BLK
        work[:, :BLK] = mat[lo:hi, lo:hi]
        work[:, BLK:] = eye
        base_inverse(work, cols, lambda: between(2 * b + 1))
        winv = work[:, BLK:]
        if hi < size:
            panel = jnp.dot(winv, mat[lo:hi, hi:size], precision=HI, preferred_element_type=jnp.float32)
        if lo > 0:
            left = jnp.dot(winv, mat[lo:hi, size : size + lo], precision=HI, preferred_element_type=jnp.float32)
            mat[lo:hi, size : size + lo] = left
        mat[lo:hi, size + lo : size + hi] = winv
        if hi < size:
            right = mat[lo:hi, size : size + hi]
            dims = (((0,), (0,)), ((), ()))
            mat[hi:size, hi:size] = mat[hi:size, hi:size] - lax.dot_general(panel, panel, dims, precision=HI, preferred_element_type=jnp.float32)
            mat[hi:size, size : size + hi] = mat[hi:size, size : size + hi] - lax.dot_general(panel, right, dims, precision=HI, preferred_element_type=jnp.float32)
        between(2 * b + 2)


def pair_blocks(size):
    count = size // BLK
    return [(i, j) for i in range(count) for j in range(i + 1)]


def kernel(
    nr, nc, t_ref, op_ref, part_ref, var_ref, inv_ref, gain_ref, xc_ref, pred_ref,
    xr_ref, acc, full, land, tland, mat, work, cols, send_sem, recv_sem,
):
    ratio = nr // nc
    row, col = lax.axis_index("row"), lax.axis_index("col")
    high, low = row // ratio, row % ratio
    packed = acc.shape[0]
    rows, size = t_ref.shape
    chunk = rows // nc
    sub = chunk // 2
    pieces = 2 * nc
    used = [0]

    def take(count):
        used[0] += count
        return used[0] - count

    levels = [
        (ratio, low, lambda d: (high * ratio + lax.rem(low + d, ratio), col)),
        (nc, col, lambda d: (row, lax.rem(col + d, nc))),
        (nc, high, lambda d: (lax.rem(high + d, nc) * ratio + low, col)),
    ]
    barrier = pltpu.get_barrier_semaphore()
    for n, me, peer in levels:
        for d in range(1, n):
            pl.semaphore_signal(barrier, inc=1, device_id=peer(d), device_id_type=MESH)
    pl.semaphore_wait(barrier, ratio - 1 + 2 * (nc - 1))

    def remote(src, dst, sem, device):
        return pltpu.make_async_remote_copy(
            src_ref=src, dst_ref=dst, send_sem=send_sem.at[sem], recv_sem=recv_sem.at[sem],
            device_id=device, device_id_type=MESH,
        )

    t_base = take(2 * (nc - 1))
    _, _, col_peer = levels[1]
    t_copies = []
    for h in range(2):
        for d in range(1, nc):
            other = lax.rem(col + d, nc)
            src = t_ref.at[pl.ds(pl.multiple_of(other * chunk + h * sub, 8), sub)]
            dst = tland.at[d - 1, pl.ds(h * sub, sub)]
            t_copies.append(remote(src, dst, t_base + h * (nc - 1) + d - 1, col_peer(d)))
    for copy in t_copies[: nc - 1]:
        copy.start()

    gather_base = take(2 * (nc - 1))
    chain_base = take(pieces)
    down_base = take(pieces)
    sib_base = take(pieces * (ratio - 1))
    gathers = []
    for h in range(2):
        for d in range(1, nc):
            own = xr_ref.at[pl.ds(pl.multiple_of(col * chunk + h * sub, 8), sub)]
            gathers.append(remote(own, own, gather_base + h * (nc - 1) + d - 1, col_peer(d)))
    _, _, low_peer = levels[0]
    source = high == col
    top = nc - 1
    above = (jnp.minimum(high + 1, top) * ratio + low, col)
    below = (jnp.maximum(high - 1, 0) * ratio + low, col)
    goes_up = jnp.logical_and(high >= col, high < top)
    goes_down = jnp.logical_and(high <= col, high > 0)
    onward = jnp.logical_or(goes_up, goes_down)
    middle = jnp.logical_and(onward, jnp.logical_not(source))
    last = jnp.logical_and(jnp.logical_not(onward), jnp.logical_not(source))

    spot = [(0, 0), (0, 1)] + [(d, h) for h in range(2) for d in range(1, nc)]

    def links(e, src_is_own):
        begin = pl.multiple_of(lax.rem(col - spot[e][0] + nc, nc) * chunk + spot[e][1] * sub, 8)
        dst = xc_ref.at[low, pl.ds(begin, sub)]
        src = xr_ref.at[pl.ds(begin, sub)] if src_is_own else dst
        up = remote(src, dst, chain_base + e, above)
        down = pltpu.make_async_remote_copy(
            src_ref=src, dst_ref=dst, send_sem=send_sem.at[down_base + e],
            recv_sem=recv_sem.at[chain_base + e], device_id=below, device_id_type=MESH,
        )
        sibs = [remote(src, dst, sib_base + e * (ratio - 1) + q - 1, low_peer(q)) for q in range(1, ratio)]
        return begin, up, down, sibs

    def send_on(up, down, sibs):
        @pl.when(goes_up)
        def _():
            up.start()

        @pl.when(goes_down)
        def _():
            down.start()

        for sib in sibs:
            sib.start()

    def relay_source(e):
        if e >= 2:
            gathers[e - 2].wait_recv()
        begin, up, down, sibs = links(e, True)
        send_on(up, down, sibs)
        xc_ref[low, pl.ds(begin, sub), :] = xr_ref[pl.ds(begin, sub), :]

    def relay_middle(e):
        begin, up, down, sibs = links(e, False)
        up.wait_recv()
        send_on(up, down, sibs)

    def relay_last(e):
        begin, up, down, sibs = links(e, False)
        up.wait_recv()
        for sib in sibs:
            sib.start()

    near = jnp.abs(high - col) == 1

    def between(slot):
        @pl.when(source)
        def _():
            if 2 <= slot + 2 < pieces:
                relay_source(slot + 2)

        @pl.when(jnp.logical_and(middle, near))
        def _():
            if slot == 0:
                relay_middle(0)
            if slot + 1 < pieces:
                relay_middle(slot + 1)

        @pl.when(jnp.logical_and(middle, jnp.logical_not(near)))
        def _():
            if 0 <= slot - 1 < pieces:
                relay_middle(slot - 1)

        @pl.when(last)
        def _():
            if 0 <= slot - 2 < pieces:
                relay_last(slot - 2)

    def owned(h):
        for copy in t_copies[h * (nc - 1) : (h + 1) * (nc - 1)]:
            copy.wait()
        where = pl.ds(pl.multiple_of(col * chunk + h * sub, 8), sub)
        total = t_ref[where, :]
        for d in range(1, nc):
            total = total + tland[d - 1, h * sub : (h + 1) * sub, :]
        xr_ref[where, :] = total

        @pl.when(source)
        def _():
            relay_source(h)

    place = 0
    for i in range(size // BLK):
        block = lax.dot_general(
            op_ref[:, i * BLK : (i + 1) * BLK], t_ref[:, : (i + 1) * BLK], (((0,), (0,)), ((), ())),
            precision=MID, preferred_element_type=jnp.float32,
        )
        for j in range(i + 1):
            acc[place : place + BLK, :] = block[:, j * BLK : (j + 1) * BLK]
            place += BLK
    acc[place : place + 8, :] = part_ref[...]
    acc[place + 8 :, :] = jnp.zeros((packed - place - 8, BLK), jnp.float32)
    start, length, slot = 0, packed, 0
    spots = []
    for level, (n, me, peer) in enumerate(levels):
        part = length // n
        base = take(n - 1)
        copies = []
        for d in range(1, n):
            other = lax.rem(me + d, n)
            src = acc.at[pl.ds(pl.multiple_of(start + other * part, 8), part)]
            dst = land.at[pl.ds(slot + (d - 1) * part, part)]
            copies.append(remote(src, dst, base + d - 1, peer(d)))
            copies[-1].start()
        if level == 1:
            for copy in t_copies[nc - 1 :]:
                copy.start()
        start = pl.multiple_of(start + me * part, 8)
        length = part
        spots.append((start, part))
        for copy in copies:
            copy.wait()
        if level == 1:
            owned(0)
        mine = acc[pl.ds(start, part), :]
        for d in range(1, n):
            mine = mine + land[pl.ds(slot + (d - 1) * part, part), :]
        acc[pl.ds(start, part), :] = mine
        slot += (n - 1) * part
    full[pl.ds(start, length), :] = acc[pl.ds(start, length), :]

    for level in (2, 1, 0):
        n, me, peer = levels[level]
        begin, part = spots[level]
        base = take(n - 1)
        copies = []
        for d in range(1, n):
            where = full.at[pl.ds(begin, part)]
            copies.append(remote(where, where, base + d - 1, peer(d)))
            copies[-1].start()
        if level == 1:
            owned(1)
            for copy in gathers:
                copy.start()
        for copy in copies:
            copy.wait()

    same = lax.broadcasted_iota(jnp.int32, (BLK, BLK), 0) == lax.broadcasted_iota(jnp.int32, (BLK, BLK), 1)
    for index, (i, j) in enumerate(pair_blocks(size)):
        block = full[index * BLK : (index + 1) * BLK, :]
        if i == j:
            block = 0.5 * (block + block.T) + jnp.where(same, var_ref[:, i * BLK : (i + 1) * BLK], 0.0)
        mat[i * BLK : (i + 1) * BLK, j * BLK : (j + 1) * BLK] = block
        if i != j:
            mat[j * BLK : (j + 1) * BLK, i * BLK : (i + 1) * BLK] = block.T
    mat[:, size:] = jnp.zeros((size, size), jnp.float32)
    tail = len(pair_blocks(size)) * BLK
    pred_ref[...] = full[tail : tail + 8, :]

    between(0)
    factor_inverse(mat, work, cols, between)
    inverse = mat[:, size:]
    inv_ref[...] = inverse
    for copy in gathers:
        copy.wait_send()

    @pl.when(jnp.logical_not(source))
    def _():
        for copy in gathers:
            copy.wait_recv()

    for slot in range(2 * (size // BLK) + 1, pieces):
        between(slot)
    gain_ref[...] = lax.dot_general(
        xr_ref[...], inverse, (((1,), (1,)), ((), ())), precision=MID, preferred_element_type=jnp.float32
    )
    for slot in range(max(pieces, 2 * (size // BLK) + 1), pieces + 2):
        between(slot)

    for e in range(pieces):
        _, up, down, sibs = links(e, False)

        @pl.when(goes_up)
        def _():
            up.wait_send()

        @pl.when(goes_down)
        def _():
            down.wait_send()

        for sib in sibs:
            sib.wait()


def exchange(mesh, total, part, row_op, part_pred, variance):
    nr, nc = mesh.shape["row"], mesh.shape["col"]
    ratio = nr // nc
    rows, size = part.shape
    landing, length = 0, total
    for n in (ratio, nc, nc):
        landing += (n - 1) * (length // n)
        length //= n
    sems = 2 * (ratio - 1 + 2 * (nc - 1)) + 4 * (nc - 1) + 4 * nc + 2 * nc * (ratio - 1)
    f32 = jnp.float32
    vmem = pl.BlockSpec(memory_space=pltpu.VMEM)
    return pl.pallas_call(
        functools.partial(kernel, nr, nc),
        out_shape=(
            jax.ShapeDtypeStruct((size, size), f32),
            jax.ShapeDtypeStruct((rows, size), f32),
            jax.ShapeDtypeStruct((ratio, rows, size), f32),
            jax.ShapeDtypeStruct((8, BLK), f32),
        ),
        in_specs=[vmem] * 4,
        out_specs=(vmem,) * 4,
        scratch_shapes=[
            pltpu.VMEM((rows, size), f32),
            pltpu.VMEM((total, BLK), f32),
            pltpu.VMEM((total, BLK), f32),
            pltpu.VMEM((landing, BLK), f32),
            pltpu.VMEM((nc - 1, rows // nc, size), f32),
            pltpu.VMEM((size, 2 * size), f32),
            pltpu.VMEM((BLK, 2 * BLK), f32),
            pltpu.VMEM((BLK, BLK), f32),
            pltpu.SemaphoreType.DMA((sems,)),
            pltpu.SemaphoreType.DMA((sems,)),
        ],
        compiler_params=pltpu.CompilerParams(collective_id=0, has_side_effects=True, vmem_limit_bytes=40 * 1024 * 1024),
    )(part, row_op, part_pred, variance)


def dot(a, b, precision):
    return jnp.dot(a, b, precision=precision, preferred_element_type=jnp.float32)


def local_operator(cells, weights, start, count):
    positions = start + lax.iota(jnp.int32, count)[:, None]
    total = jnp.zeros((count, cells.shape[1]), jnp.float32)
    for foot in range(cells.shape[0]):
        total = total + jnp.where(cells[foot][None, :] == positions, weights[foot][None, :], 0.0)
    return total


def on_device(mesh, covariance, state_mean, obs_values, obs_cells, obs_weights, obs_variance):
    rows_dev, cols_dev = covariance.shape
    row_index = lax.axis_index("row")
    col_index = lax.axis_index("col")
    devices = mesh.shape["row"] * mesh.shape["col"]
    batches, foot, width = obs_cells.shape
    total = batches * width
    cells = obs_cells.transpose(1, 0, 2).reshape(foot, total)
    weights = obs_weights.transpose(1, 0, 2).reshape(foot, total)
    values = obs_values.reshape(total)
    variance = obs_variance.reshape(1, total)
    col_op = local_operator(cells, weights, col_index * cols_dev, cols_dev)
    row_op = local_operator(cells, weights, row_index * rows_dev, rows_dev)
    part = dot(covariance, col_op, MID)
    part_pred = jnp.sum(row_op * state_mean[:, None], axis=0)
    part_pred = jnp.where(col_index == 0, part_pred, 0.0).reshape(total // BLK, BLK)
    part_pred = jnp.pad(part_pred, ((0, 8 - total // BLK), (0, 0)))
    filled = len(pair_blocks(total)) * BLK + 8
    unit = 8 * devices
    packed = -(-(filled + 8) // unit) * unit
    inverse, gain, cross_cols, pred = exchange(mesh, packed, part, row_op, part_pred, variance)
    predicted = pred[: total // BLK].reshape(total)
    innov = values - predicted
    white = jnp.sum(inverse * innov[None, :], axis=1)
    gain_cols = dot(cross_cols.reshape(cols_dev, total), inverse.T, MID)
    mean = state_mean + jnp.sum(gain * white[None, :], axis=1)
    matrix = covariance - dot(gain, gain_cols.T, MID)
    return (matrix, mean)


def solution(mesh):
    return jax.shard_map(
        functools.partial(on_device, mesh),
        mesh=mesh,
        in_specs=(P("row", "col"), P("row"), P(), P(), P(), P()),
        out_specs=(P("row", "col"), P("row")),
        check_vma=False,
    )
```

```python
import functools

import jax
import jax.numpy as jnp
from jax import lax
from jax.experimental import pallas as pl
from jax.experimental.pallas import tpu as pltpu
from jax.sharding import PartitionSpec as P

HI = lax.Precision.HIGHEST
MID = lax.Precision.HIGH
MESH = pl.DeviceIdType.MESH
BLK = 128
SUB = 8

def base_inverse(work, cols, midway):
    def panel_step(first, g, carry):
        start = pl.multiple_of(g * SUB, SUB)
        panel = work[pl.ds(start, SUB), :]
        square = pltpu.roll(panel[:, :BLK], BLK - start, 1)[:, :SUB]
        wide = [jnp.broadcast_to(square[:, j : j + 1], (SUB, BLK)) for j in range(SUB)]
        left, right = panel[:, :BLK], panel[:, BLK:]
        below = lax.broadcasted_iota(jnp.int32, (SUB, BLK), 0)
        scale = jnp.zeros((SUB, BLK), jnp.float32)
        for j in range(SUB):
            pivot = jnp.broadcast_to(wide[j][j : j + 1, :], (SUB, BLK))
            inv = 1.0 / pivot
            scale = jnp.where(below == j, lax.rsqrt(pivot), scale)
            ratio = jnp.where(below > j, wide[j] * inv, 0.0)
            left = left - ratio * left[j : j + 1, :]
            right = right - ratio * right[j : j + 1, :]
            for k in range(j + 1, SUB):
                wide[k] = wide[k] - ratio * wide[k][j : j + 1, :]
        left = left * scale
        right = right * scale
        both = jnp.concatenate([left, right], axis=1)
        lane = lax.broadcasted_iota(jnp.int32, (SUB, BLK), 1)
        lhs = jnp.where(lane >= start + SUB, left, 0.0)
        work[pl.ds(start, SUB), :] = both
        work[first:, :] = work[first:, :] - lax.dot_general(lhs[:, first:], both, (((0,), (0,)), ((), ())), precision=HI, preferred_element_type=jnp.float32)
        return carry
    steps = BLK // SUB // 4
    for quarter in range(4):
        if quarter == 2:
            midway()
        first = quarter * steps * SUB
        lax.fori_loop(quarter * steps, (quarter + 1) * steps, functools.partial(panel_step, first), 0)

def factor_inverse(mat, work, cols, between):
    size = mat.shape[0]
    eye = (lax.broadcasted_iota(jnp.int32, (BLK, BLK), 0) == lax.broadcasted_iota(jnp.int32, (BLK, BLK), 1)).astype(jnp.float32)
    for b in range(size // BLK):
        lo, hi = b * BLK, (b + 1) * BLK
        work[:, :BLK] = mat[lo:hi, lo:hi]
        work[:, BLK:] = eye
        base_inverse(work, cols, lambda: between(2 * b + 1))
        winv = work[:, BLK:]
        if hi < size:
            panel = jnp.dot(winv, mat[lo:hi, hi:size], precision=HI, preferred_element_type=jnp.float32)
        if lo > 0:
            left = jnp.dot(winv, mat[lo:hi, size : size + lo], precision=HI, preferred_element_type=jnp.float32)
            mat[lo:hi, size : size + lo] = left
        mat[lo:hi, size + lo : size + hi] = winv
        if hi < size:
            right = mat[lo:hi, size : size + hi]
            dims = (((0,), (0,)), ((), ()))
            mat[hi:size, hi:size] = mat[hi:size, hi:size] - lax.dot_general(panel, panel, dims, precision=HI, preferred_element_type=jnp.float32)
            mat[hi:size, size : size + hi] = mat[hi:size, size : size + hi] - lax.dot_general(panel, right, dims, precision=HI, preferred_element_type=jnp.float32)
        between(2 * b + 2)


def pair_blocks(size):
    count = size // BLK
    return [(i, j) for i in range(count) for j in range(i + 1)]


def kernel(
    nr, nc, t_ref, op_ref, part_ref, var_ref, inv_ref, gain_ref, xc_ref, pred_ref,
    xr_ref, acc, full, land, tland, mat, work, cols, send_sem, recv_sem,
):
    ratio = nr // nc
    row, col = lax.axis_index("row"), lax.axis_index("col")
    high, low = row // ratio, row % ratio
    packed = acc.shape[0]
    rows, size = t_ref.shape
    chunk = rows // nc
    sub = chunk // 2
    pieces = 2 * nc
    used = [0]

    def take(count):
        used[0] += count
        return used[0] - count

    levels = [
        (ratio, low, lambda d: (high * ratio + lax.rem(low + d, ratio), col)),
        (nc, col, lambda d: (row, lax.rem(col + d, nc))),
        (nc, high, lambda d: (lax.rem(high + d, nc) * ratio + low, col)),
    ]
    barrier = pltpu.get_barrier_semaphore()
    for n, me, peer in levels:
        for d in range(1, n):
            pl.semaphore_signal(barrier, inc=1, device_id=peer(d), device_id_type=MESH)
    pl.semaphore_wait(barrier, ratio - 1 + 2 * (nc - 1))

    def remote(src, dst, sem, device):
        return pltpu.make_async_remote_copy(
            src_ref=src, dst_ref=dst, send_sem=send_sem.at[sem], recv_sem=recv_sem.at[sem],
            device_id=device, device_id_type=MESH,
        )

    t_base = take(2 * (nc - 1))
    _, _, col_peer = levels[1]
    t_copies = []
    for h in range(2):
        for d in range(1, nc):
            other = lax.rem(col + d, nc)
            src = t_ref.at[pl.ds(pl.multiple_of(other * chunk + h * sub, 8), sub)]
            dst = tland.at[d - 1, pl.ds(h * sub, sub)]
            t_copies.append(remote(src, dst, t_base + h * (nc - 1) + d - 1, col_peer(d)))
    for copy in t_copies[: nc - 1]:
        copy.start()

    gather_base = take(2 * (nc - 1))
    chain_base = take(pieces)
    down_base = take(pieces)
    sib_base = take(pieces * (ratio - 1))
    gathers = []
    for h in range(2):
        for d in range(1, nc):
            own = xr_ref.at[pl.ds(pl.multiple_of(col * chunk + h * sub, 8), sub)]
            gathers.append(remote(own, own, gather_base + h * (nc - 1) + d - 1, col_peer(d)))
    _, _, low_peer = levels[0]
    source = high == col
    top = nc - 1
    above = (jnp.minimum(high + 1, top) * ratio + low, col)
    below = (jnp.maximum(high - 1, 0) * ratio + low, col)
    goes_up = jnp.logical_and(high >= col, high < top)
    goes_down = jnp.logical_and(high <= col, high > 0)
    onward = jnp.logical_or(goes_up, goes_down)
    middle = jnp.logical_and(onward, jnp.logical_not(source))
    last = jnp.logical_and(jnp.logical_not(onward), jnp.logical_not(source))

    spot = [(0, 0), (0, 1)] + [(d, h) for h in range(2) for d in range(1, nc)]

    def links(e, src_is_own):
        begin = pl.multiple_of(lax.rem(col - spot[e][0] + nc, nc) * chunk + spot[e][1] * sub, 8)
        dst = xc_ref.at[low, pl.ds(begin, sub)]
        src = xr_ref.at[pl.ds(begin, sub)] if src_is_own else dst
        up = remote(src, dst, chain_base + e, above)
        down = pltpu.make_async_remote_copy(
            src_ref=src, dst_ref=dst, send_sem=send_sem.at[down_base + e],
            recv_sem=recv_sem.at[chain_base + e], device_id=below, device_id_type=MESH,
        )
        sibs = [remote(src, dst, sib_base + e * (ratio - 1) + q - 1, low_peer(q)) for q in range(1, ratio)]
        return begin, up, down, sibs

    def send_on(up, down, sibs):
        @pl.when(goes_up)
        def _():
            up.start()

        @pl.when(goes_down)
        def _():
            down.start()

        for sib in sibs:
            sib.start()

    def relay_source(e):
        if e >= 2:
            gathers[e - 2].wait_recv()
        begin, up, down, sibs = links(e, True)
        send_on(up, down, sibs if e >= 2 else [])
        xc_ref[low, pl.ds(begin, sub), :] = xr_ref[pl.ds(begin, sub), :]

    def relay_middle(e):
        begin, up, down, sibs = links(e, False)
        up.wait_recv()
        send_on(up, down, sibs)

    def relay_last(e):
        begin, up, down, sibs = links(e, False)
        up.wait_recv()
        for sib in sibs:
            sib.start()

    near = jnp.abs(high - col) == 1

    def between(slot):
        @pl.when(source)
        def _():
            if slot == 0:
                for e in range(2):
                    for sib in links(e, True)[3]:
                        sib.start()
            if 2 <= slot + 2 < pieces:
                relay_source(slot + 2)

        @pl.when(jnp.logical_and(middle, near))
        def _():
            if slot == 0:
                relay_middle(0)
            if slot + 1 < pieces:
                relay_middle(slot + 1)

        @pl.when(jnp.logical_and(middle, jnp.logical_not(near)))
        def _():
            if 0 <= slot - 1 < pieces:
                relay_middle(slot - 1)

        @pl.when(last)
        def _():
            if 0 <= slot - 2 < pieces:
                relay_last(slot - 2)

    def owned(h):
        for copy in t_copies[h * (nc - 1) : (h + 1) * (nc - 1)]:
            copy.wait()
        where = pl.ds(pl.multiple_of(col * chunk + h * sub, 8), sub)
        total = t_ref[where, :]
        for d in range(1, nc):
            total = total + tland[d - 1, h * sub : (h + 1) * sub, :]
        xr_ref[where, :] = total

        @pl.when(source)
        def _():
            relay_source(h)

    place = 0
    for i in range(size // BLK):
        block = lax.dot_general(
            op_ref[:, i * BLK : (i + 1) * BLK], t_ref[:, : (i + 1) * BLK], (((0,), (0,)), ((), ())),
            precision=MID, preferred_element_type=jnp.float32,
        )
        for j in range(i + 1):
            acc[place : place + BLK, :] = block[:, j * BLK : (j + 1) * BLK]
            place += BLK
    acc[place : place + 8, :] = part_ref[...]
    acc[place + 8 :, :] = jnp.zeros((packed - place - 8, BLK), jnp.float32)
    start, length, slot = 0, packed, 0
    spots = []
    for level, (n, me, peer) in enumerate(levels):
        part = length // n
        base = take(n - 1)
        copies = []
        for d in range(1, n):
            other = lax.rem(me + d, n)
            src = acc.at[pl.ds(pl.multiple_of(start + other * part, 8), part)]
            dst = land.at[pl.ds(slot + (d - 1) * part, part)]
            copies.append(remote(src, dst, base + d - 1, peer(d)))
            copies[-1].start()
        if level == 1:
            for copy in t_copies[nc - 1 :]:
                copy.start()
        start = pl.multiple_of(start + me * part, 8)
        length = part
        spots.append((start, part))
        for copy in copies:
            copy.wait()
        mine = acc[pl.ds(start, part), :]
        for d in range(1, n):
            mine = mine + land[pl.ds(slot + (d - 1) * part, part), :]
        acc[pl.ds(start, part), :] = mine
        slot += (n - 1) * part
    full[pl.ds(start, length), :] = acc[pl.ds(start, length), :]

    for level in (2, 1, 0):
        n, me, peer = levels[level]
        begin, part = spots[level]
        base = take(n - 1)
        copies = []
        for d in range(1, n):
            where = full.at[pl.ds(begin, part)]
            copies.append(remote(where, where, base + d - 1, peer(d)))
            copies[-1].start()
        if level == 1:
            owned(1)
            for copy in gathers:
                copy.start()
        for copy in copies:
            copy.wait()
        if level == 2:
            owned(0)

    same = lax.broadcasted_iota(jnp.int32, (BLK, BLK), 0) == lax.broadcasted_iota(jnp.int32, (BLK, BLK), 1)
    for index, (i, j) in enumerate(pair_blocks(size)):
        block = full[index * BLK : (index + 1) * BLK, :]
        if i == j:
            block = 0.5 * (block + block.T) + jnp.where(same, var_ref[:, i * BLK : (i + 1) * BLK], 0.0)
        mat[i * BLK : (i + 1) * BLK, j * BLK : (j + 1) * BLK] = block
        if i != j:
            mat[j * BLK : (j + 1) * BLK, i * BLK : (i + 1) * BLK] = block.T
    mat[:, size:] = jnp.zeros((size, size), jnp.float32)
    tail = len(pair_blocks(size)) * BLK
    pred_ref[...] = full[tail : tail + 8, :]

    between(0)
    factor_inverse(mat, work, cols, between)
    inverse = mat[:, size:]
    inv_ref[...] = inverse
    for copy in gathers:
        copy.wait_send()

    @pl.when(jnp.logical_not(source))
    def _():
        for copy in gathers:
            copy.wait_recv()

    for slot in range(2 * (size // BLK) + 1, pieces):
        between(slot)
    gain_ref[...] = lax.dot_general(
        xr_ref[...], inverse, (((1,), (1,)), ((), ())), precision=MID, preferred_element_type=jnp.float32
    )
    for slot in range(max(pieces, 2 * (size // BLK) + 1), pieces + 2):
        between(slot)

    for e in range(pieces):
        _, up, down, sibs = links(e, False)

        @pl.when(goes_up)
        def _():
            up.wait_send()

        @pl.when(goes_down)
        def _():
            down.wait_send()

        for sib in sibs:
            sib.wait()


def exchange(mesh, total, part, row_op, part_pred, variance):
    nr, nc = mesh.shape["row"], mesh.shape["col"]
    ratio = nr // nc
    rows, size = part.shape
    landing, length = 0, total
    for n in (ratio, nc, nc):
        landing += (n - 1) * (length // n)
        length //= n
    sems = 2 * (ratio - 1 + 2 * (nc - 1)) + 4 * (nc - 1) + 4 * nc + 2 * nc * (ratio - 1)
    f32 = jnp.float32
    vmem = pl.BlockSpec(memory_space=pltpu.VMEM)
    return pl.pallas_call(
        functools.partial(kernel, nr, nc),
        out_shape=(
            jax.ShapeDtypeStruct((size, size), f32),
            jax.ShapeDtypeStruct((rows, size), f32),
            jax.ShapeDtypeStruct((ratio, rows, size), f32),
            jax.ShapeDtypeStruct((8, BLK), f32),
        ),
        in_specs=[vmem] * 4,
        out_specs=(vmem,) * 4,
        scratch_shapes=[
            pltpu.VMEM((rows, size), f32),
            pltpu.VMEM((total, BLK), f32),
            pltpu.VMEM((total, BLK), f32),
            pltpu.VMEM((landing, BLK), f32),
            pltpu.VMEM((nc - 1, rows // nc, size), f32),
            pltpu.VMEM((size, 2 * size), f32),
            pltpu.VMEM((BLK, 2 * BLK), f32),
            pltpu.VMEM((BLK, BLK), f32),
            pltpu.SemaphoreType.DMA((sems,)),
            pltpu.SemaphoreType.DMA((sems,)),
        ],
        compiler_params=pltpu.CompilerParams(collective_id=0, has_side_effects=True, vmem_limit_bytes=40 * 1024 * 1024),
    )(part, row_op, part_pred, variance)


def dot(a, b, precision):
    return jnp.dot(a, b, precision=precision, preferred_element_type=jnp.float32)


def local_operator(cells, weights, start, count):
    positions = start + lax.iota(jnp.int32, count)[:, None]
    total = jnp.zeros((count, cells.shape[1]), jnp.float32)
    for foot in range(cells.shape[0]):
        total = total + jnp.where(cells[foot][None, :] == positions, weights[foot][None, :], 0.0)
    return total


def on_device(mesh, covariance, state_mean, obs_values, obs_cells, obs_weights, obs_variance):
    rows_dev, cols_dev = covariance.shape
    row_index = lax.axis_index("row")
    col_index = lax.axis_index("col")
    devices = mesh.shape["row"] * mesh.shape["col"]
    batches, foot, width = obs_cells.shape
    total = batches * width
    cells = obs_cells.transpose(1, 0, 2).reshape(foot, total)
    weights = obs_weights.transpose(1, 0, 2).reshape(foot, total)
    values = obs_values.reshape(total)
    variance = obs_variance.reshape(1, total)
    col_op = local_operator(cells, weights, col_index * cols_dev, cols_dev)
    row_op = local_operator(cells, weights, row_index * rows_dev, rows_dev)
    part = dot(covariance, col_op, MID)
    part_pred = jnp.sum(row_op * state_mean[:, None], axis=0)
    part_pred = jnp.where(col_index == 0, part_pred, 0.0).reshape(total // BLK, BLK)
    part_pred = jnp.pad(part_pred, ((0, 8 - total // BLK), (0, 0)))
    filled = len(pair_blocks(total)) * BLK + 8
    unit = 8 * devices
    packed = -(-(filled + 8) // unit) * unit
    inverse, gain, cross_cols, pred = exchange(mesh, packed, part, row_op, part_pred, variance)
    predicted = pred[: total // BLK].reshape(total)
    innov = values - predicted
    white = jnp.sum(inverse * innov[None, :], axis=1)
    gain_cols = dot(cross_cols.reshape(cols_dev, total), inverse.T, MID)
    mean = state_mean + jnp.sum(gain * white[None, :], axis=1)
    matrix = covariance - dot(gain, gain_cols.T, MID)
    return (matrix, mean)


def solution(mesh):
    return jax.shard_map(
        functools.partial(on_device, mesh),
        mesh=mesh,
        in_specs=(P("row", "col"), P("row"), P(), P(), P(), P()),
        out_specs=(P("row", "col"), P("row")),
        check_vma=False,
    )
```

```python
import functools

import jax
import jax.numpy as jnp
from jax import lax
from jax.experimental import pallas as pl
from jax.experimental.pallas import tpu as pltpu
from jax.sharding import PartitionSpec as P

HI = lax.Precision.HIGHEST
MID = lax.Precision.HIGH
MESH = pl.DeviceIdType.MESH
BLK = 128
SUB = 8

def base_inverse(work, cols, midway):
    def panel_step(first, g, carry):
        start = pl.multiple_of(g * SUB, SUB)
        panel = work[pl.ds(start, SUB), :]
        square = pltpu.roll(panel[:, :BLK], BLK - start, 1)[:, :SUB]
        wide = [jnp.broadcast_to(square[:, j : j + 1], (SUB, BLK)) for j in range(SUB)]
        left, right = panel[:, :BLK], panel[:, BLK:]
        below = lax.broadcasted_iota(jnp.int32, (SUB, BLK), 0)
        scale = jnp.zeros((SUB, BLK), jnp.float32)
        for j in range(SUB):
            pivot = jnp.broadcast_to(wide[j][j : j + 1, :], (SUB, BLK))
            inv = 1.0 / pivot
            scale = jnp.where(below == j, lax.rsqrt(pivot), scale)
            ratio = jnp.where(below > j, wide[j] * inv, 0.0)
            left = left - ratio * left[j : j + 1, :]
            right = right - ratio * right[j : j + 1, :]
            for k in range(j + 1, SUB):
                wide[k] = wide[k] - ratio * wide[k][j : j + 1, :]
        left = left * scale
        right = right * scale
        both = jnp.concatenate([left, right], axis=1)
        lane = lax.broadcasted_iota(jnp.int32, (SUB, BLK), 1)
        lhs = jnp.where(lane >= start + SUB, left, 0.0)
        work[pl.ds(start, SUB), :] = both
        work[first:, :] = work[first:, :] - lax.dot_general(lhs[:, first:], both, (((0,), (0,)), ((), ())), precision=HI, preferred_element_type=jnp.float32)
        return carry
    steps = BLK // SUB // 4
    for quarter in range(4):
        if quarter == 2:
            midway()
        first = quarter * steps * SUB
        lax.fori_loop(quarter * steps, (quarter + 1) * steps, functools.partial(panel_step, first), 0)

def factor_inverse(mat, work, cols, between):
    size = mat.shape[0]
    eye = (lax.broadcasted_iota(jnp.int32, (BLK, BLK), 0) == lax.broadcasted_iota(jnp.int32, (BLK, BLK), 1)).astype(jnp.float32)
    for b in range(size // BLK):
        lo, hi = b * BLK, (b + 1) * BLK
        work[:, :BLK] = mat[lo:hi, lo:hi]
        work[:, BLK:] = eye
        base_inverse(work, cols, lambda: between(2 * b + 1))
        winv = work[:, BLK:]
        if hi < size:
            panel = jnp.dot(winv, mat[lo:hi, hi:size], precision=HI, preferred_element_type=jnp.float32)
        if lo > 0:
            left = jnp.dot(winv, mat[lo:hi, size : size + lo], precision=HI, preferred_element_type=jnp.float32)
            mat[lo:hi, size : size + lo] = left
        mat[lo:hi, size + lo : size + hi] = winv
        if hi < size:
            right = mat[lo:hi, size : size + hi]
            dims = (((0,), (0,)), ((), ()))
            mat[hi:size, hi:size] = mat[hi:size, hi:size] - lax.dot_general(panel, panel, dims, precision=HI, preferred_element_type=jnp.float32)
            mat[hi:size, size : size + hi] = mat[hi:size, size : size + hi] - lax.dot_general(panel, right, dims, precision=HI, preferred_element_type=jnp.float32)
        between(2 * b + 2)


def pair_blocks(size):
    count = size // BLK
    return [(i, j) for i in range(count) for j in range(i + 1)]


def kernel(
    nr, nc, t_ref, op_ref, part_ref, var_ref, inv_ref, gain_ref, xc_ref, pred_ref,
    xr_ref, acc, full, land, tland, mat, work, cols, send_sem, recv_sem,
):
    ratio = nr // nc
    row, col = lax.axis_index("row"), lax.axis_index("col")
    high, low = row // ratio, row % ratio
    packed = acc.shape[0]
    rows, size = t_ref.shape
    chunk = rows // nc
    sub = chunk // 2
    pieces = 2 * nc
    used = [0]

    def take(count):
        used[0] += count
        return used[0] - count

    levels = [
        (ratio, low, lambda d: (high * ratio + lax.rem(low + d, ratio), col)),
        (nc, col, lambda d: (row, lax.rem(col + d, nc))),
        (nc, high, lambda d: (lax.rem(high + d, nc) * ratio + low, col)),
    ]
    barrier = pltpu.get_barrier_semaphore()
    for n, me, peer in levels:
        for d in range(1, n):
            pl.semaphore_signal(barrier, inc=1, device_id=peer(d), device_id_type=MESH)
    pl.semaphore_wait(barrier, ratio - 1 + 2 * (nc - 1))

    def remote(src, dst, sem, device):
        return pltpu.make_async_remote_copy(
            src_ref=src, dst_ref=dst, send_sem=send_sem.at[sem], recv_sem=recv_sem.at[sem],
            device_id=device, device_id_type=MESH,
        )

    t_base = take(2 * (nc - 1))
    _, _, col_peer = levels[1]
    t_copies = []
    for h in range(2):
        for d in range(1, nc):
            other = lax.rem(col + d, nc)
            src = t_ref.at[pl.ds(pl.multiple_of(other * chunk + h * sub, 8), sub)]
            dst = tland.at[d - 1, pl.ds(h * sub, sub)]
            t_copies.append(remote(src, dst, t_base + h * (nc - 1) + d - 1, col_peer(d)))
    for copy in t_copies[: nc - 1]:
        copy.start()

    gather_base = take(2 * (nc - 1))
    chain_base = take(pieces)
    down_base = take(pieces)
    sib_base = take(pieces * (ratio - 1))
    gathers = []
    for h in range(2):
        for d in range(1, nc):
            own = xr_ref.at[pl.ds(pl.multiple_of(col * chunk + h * sub, 8), sub)]
            gathers.append(remote(own, own, gather_base + h * (nc - 1) + d - 1, col_peer(d)))
    _, _, low_peer = levels[0]
    source = high == col
    top = nc - 1
    above = (jnp.minimum(high + 1, top) * ratio + low, col)
    below = (jnp.maximum(high - 1, 0) * ratio + low, col)
    goes_up = jnp.logical_and(high >= col, high < top)
    goes_down = jnp.logical_and(high <= col, high > 0)
    onward = jnp.logical_or(goes_up, goes_down)
    middle = jnp.logical_and(onward, jnp.logical_not(source))
    last = jnp.logical_and(jnp.logical_not(onward), jnp.logical_not(source))

    spot = [(0, 0), (0, 1)] + [(d, h) for h in range(2) for d in range(1, nc)]

    def links(e, src_is_own):
        begin = pl.multiple_of(lax.rem(col - spot[e][0] + nc, nc) * chunk + spot[e][1] * sub, 8)
        dst = xc_ref.at[low, pl.ds(begin, sub)]
        src = xr_ref.at[pl.ds(begin, sub)] if src_is_own else dst
        up = remote(src, dst, chain_base + e, above)
        down = pltpu.make_async_remote_copy(
            src_ref=src, dst_ref=dst, send_sem=send_sem.at[down_base + e],
            recv_sem=recv_sem.at[chain_base + e], device_id=below, device_id_type=MESH,
        )
        sibs = [remote(src, dst, sib_base + e * (ratio - 1) + q - 1, low_peer(q)) for q in range(1, ratio)]
        return begin, up, down, sibs

    def send_on(up, down, sibs):
        @pl.when(goes_up)
        def _():
            up.start()

        @pl.when(goes_down)
        def _():
            down.start()

        for sib in sibs:
            sib.start()

    def relay_source(e):
        if e >= 2:
            gathers[e - 2].wait_recv()
        begin, up, down, sibs = links(e, True)
        send_on(up, down, sibs if e >= 2 else [])
        xc_ref[low, pl.ds(begin, sub), :] = xr_ref[pl.ds(begin, sub), :]

    def relay_middle(e):
        begin, up, down, sibs = links(e, False)
        up.wait_recv()
        send_on(up, down, sibs)

    def relay_last(e):
        begin, up, down, sibs = links(e, False)
        up.wait_recv()
        for sib in sibs:
            sib.start()

    near = jnp.abs(high - col) == 1

    def between(slot):
        @pl.when(source)
        def _():
            if slot == 0:
                for e in range(2):
                    for sib in links(e, True)[3]:
                        sib.start()
                relay_source(2)
            if slot + 3 < pieces:
                relay_source(slot + 3)

        @pl.when(jnp.logical_and(middle, near))
        def _():
            if slot == 0:
                relay_middle(0)
            if slot + 1 < pieces:
                relay_middle(slot + 1)

        @pl.when(jnp.logical_and(middle, jnp.logical_not(near)))
        def _():
            if 0 <= slot - 1 < pieces - 1:
                relay_middle(slot - 1)
            if slot == pieces - 1:
                relay_middle(pieces - 1)

        @pl.when(last)
        def _():
            if 0 <= slot - 2 < pieces:
                relay_last(slot - 2)

    def owned(h):
        for copy in t_copies[h * (nc - 1) : (h + 1) * (nc - 1)]:
            copy.wait()
        where = pl.ds(pl.multiple_of(col * chunk + h * sub, 8), sub)
        total = t_ref[where, :]
        for d in range(1, nc):
            total = total + tland[d - 1, h * sub : (h + 1) * sub, :]
        xr_ref[where, :] = total

        @pl.when(source)
        def _():
            relay_source(h)

    place = 0
    for i in range(size // BLK):
        block = lax.dot_general(
            op_ref[:, i * BLK : (i + 1) * BLK], t_ref[:, : (i + 1) * BLK], (((0,), (0,)), ((), ())),
            precision=MID, preferred_element_type=jnp.float32,
        )
        for j in range(i + 1):
            acc[place : place + BLK, :] = block[:, j * BLK : (j + 1) * BLK]
            place += BLK
    acc[place : place + 8, :] = part_ref[...]
    acc[place + 8 :, :] = jnp.zeros((packed - place - 8, BLK), jnp.float32)
    start, length, slot = 0, packed, 0
    spots = []
    for level, (n, me, peer) in enumerate(levels):
        part = length // n
        base = take(n - 1)
        copies = []
        for d in range(1, n):
            other = lax.rem(me + d, n)
            src = acc.at[pl.ds(pl.multiple_of(start + other * part, 8), part)]
            dst = land.at[pl.ds(slot + (d - 1) * part, part)]
            copies.append(remote(src, dst, base + d - 1, peer(d)))
            copies[-1].start()
        if level == 1:
            for copy in t_copies[nc - 1 :]:
                copy.start()
        start = pl.multiple_of(start + me * part, 8)
        length = part
        spots.append((start, part))
        for copy in copies:
            copy.wait()
        mine = acc[pl.ds(start, part), :]
        for d in range(1, n):
            mine = mine + land[pl.ds(slot + (d - 1) * part, part), :]
        acc[pl.ds(start, part), :] = mine
        slot += (n - 1) * part
    full[pl.ds(start, length), :] = acc[pl.ds(start, length), :]

    for level in (2, 1, 0):
        n, me, peer = levels[level]
        begin, part = spots[level]
        base = take(n - 1)
        copies = []
        for d in range(1, n):
            where = full.at[pl.ds(begin, part)]
            copies.append(remote(where, where, base + d - 1, peer(d)))
            copies[-1].start()
        if level == 1:
            owned(1)
            for copy in gathers:
                copy.start()
        for copy in copies:
            copy.wait()
        if level == 2:
            owned(0)

    same = lax.broadcasted_iota(jnp.int32, (BLK, BLK), 0) == lax.broadcasted_iota(jnp.int32, (BLK, BLK), 1)
    for index, (i, j) in enumerate(pair_blocks(size)):
        block = full[index * BLK : (index + 1) * BLK, :]
        if i == j:
            block = 0.5 * (block + block.T) + jnp.where(same, var_ref[:, i * BLK : (i + 1) * BLK], 0.0)
        mat[i * BLK : (i + 1) * BLK, j * BLK : (j + 1) * BLK] = block
        if i != j:
            mat[j * BLK : (j + 1) * BLK, i * BLK : (i + 1) * BLK] = block.T
    mat[:, size:] = jnp.zeros((size, size), jnp.float32)
    tail = len(pair_blocks(size)) * BLK
    pred_ref[...] = full[tail : tail + 8, :]

    between(0)
    factor_inverse(mat, work, cols, between)
    inverse = mat[:, size:]
    inv_ref[...] = inverse
    for copy in gathers:
        copy.wait_send()

    @pl.when(jnp.logical_not(source))
    def _():
        for copy in gathers:
            copy.wait_recv()

    for slot in range(2 * (size // BLK) + 1, pieces):
        between(slot)
    gain_ref[...] = lax.dot_general(
        xr_ref[...], inverse, (((1,), (1,)), ((), ())), precision=MID, preferred_element_type=jnp.float32
    )
    for slot in range(max(pieces, 2 * (size // BLK) + 1), pieces + 2):
        between(slot)

    for e in range(pieces):
        _, up, down, sibs = links(e, False)

        @pl.when(goes_up)
        def _():
            up.wait_send()

        @pl.when(goes_down)
        def _():
            down.wait_send()

        for sib in sibs:
            sib.wait()


def exchange(mesh, total, part, row_op, part_pred, variance):
    nr, nc = mesh.shape["row"], mesh.shape["col"]
    ratio = nr // nc
    rows, size = part.shape
    landing, length = 0, total
    for n in (ratio, nc, nc):
        landing += (n - 1) * (length // n)
        length //= n
    sems = 2 * (ratio - 1 + 2 * (nc - 1)) + 4 * (nc - 1) + 4 * nc + 2 * nc * (ratio - 1)
    f32 = jnp.float32
    vmem = pl.BlockSpec(memory_space=pltpu.VMEM)
    return pl.pallas_call(
        functools.partial(kernel, nr, nc),
        out_shape=(
            jax.ShapeDtypeStruct((size, size), f32),
            jax.ShapeDtypeStruct((rows, size), f32),
            jax.ShapeDtypeStruct((ratio, rows, size), f32),
            jax.ShapeDtypeStruct((8, BLK), f32),
        ),
        in_specs=[vmem] * 4,
        out_specs=(vmem,) * 4,
        scratch_shapes=[
            pltpu.VMEM((rows, size), f32),
            pltpu.VMEM((total, BLK), f32),
            pltpu.VMEM((total, BLK), f32),
            pltpu.VMEM((landing, BLK), f32),
            pltpu.VMEM((nc - 1, rows // nc, size), f32),
            pltpu.VMEM((size, 2 * size), f32),
            pltpu.VMEM((BLK, 2 * BLK), f32),
            pltpu.VMEM((BLK, BLK), f32),
            pltpu.SemaphoreType.DMA((sems,)),
            pltpu.SemaphoreType.DMA((sems,)),
        ],
        compiler_params=pltpu.CompilerParams(collective_id=0, has_side_effects=True, vmem_limit_bytes=40 * 1024 * 1024),
    )(part, row_op, part_pred, variance)


def dot(a, b, precision):
    return jnp.dot(a, b, precision=precision, preferred_element_type=jnp.float32)


def local_operator(cells, weights, start, count):
    positions = start + lax.iota(jnp.int32, count)[:, None]
    total = jnp.zeros((count, cells.shape[1]), jnp.float32)
    for foot in range(cells.shape[0]):
        total = total + jnp.where(cells[foot][None, :] == positions, weights[foot][None, :], 0.0)
    return total


def on_device(mesh, covariance, state_mean, obs_values, obs_cells, obs_weights, obs_variance):
    rows_dev, cols_dev = covariance.shape
    row_index = lax.axis_index("row")
    col_index = lax.axis_index("col")
    devices = mesh.shape["row"] * mesh.shape["col"]
    batches, foot, width = obs_cells.shape
    total = batches * width
    cells = obs_cells.transpose(1, 0, 2).reshape(foot, total)
    weights = obs_weights.transpose(1, 0, 2).reshape(foot, total)
    values = obs_values.reshape(total)
    variance = obs_variance.reshape(1, total)
    col_op = local_operator(cells, weights, col_index * cols_dev, cols_dev)
    row_op = local_operator(cells, weights, row_index * rows_dev, rows_dev)
    part = dot(covariance, col_op, MID)
    part_pred = jnp.sum(row_op * state_mean[:, None], axis=0)
    part_pred = jnp.where(col_index == 0, part_pred, 0.0).reshape(total // BLK, BLK)
    part_pred = jnp.pad(part_pred, ((0, 8 - total // BLK), (0, 0)))
    filled = len(pair_blocks(total)) * BLK + 8
    unit = 8 * devices
    packed = -(-(filled + 8) // unit) * unit
    inverse, gain, cross_cols, pred = exchange(mesh, packed, part, row_op, part_pred, variance)
    predicted = pred[: total // BLK].reshape(total)
    innov = values - predicted
    white = jnp.sum(inverse * innov[None, :], axis=1)
    gain_cols = dot(cross_cols.reshape(cols_dev, total), inverse.T, MID)
    mean = state_mean + jnp.sum(gain * white[None, :], axis=1)
    matrix = covariance - dot(gain, gain_cols.T, MID)
    return (matrix, mean)


def solution(mesh):
    return jax.shard_map(
        functools.partial(on_device, mesh),
        mesh=mesh,
        in_specs=(P("row", "col"), P("row"), P(), P(), P(), P()),
        out_specs=(P("row", "col"), P("row")),
        check_vma=False,
    )
```
